512 devices in a mesh: leaf: 128 (over y, z, core), sub: 4 (over x).
Axes of the slice: x: 4, y: 8, z: 8, core: 2. Of those that a mesh axis runs over, the one named last changes fastest.
Arguments:
- field: float32 [64, 524288], P(None, ('leaf', 'sub')), may hold values from -6 to 6
- coords: float32 [3, 524288], P(None, ('leaf', 'sub')), may hold values from -6 to 6
- basis: float32 [2048, 64, 256], P(('leaf', 'sub')), may hold values from -0.375 to 0.375
- up_transfer: float32 [2048, 64, 64], P(('leaf', 'sub')), may hold values from -0.1875 to 0.1875
- down_transfer: float32 [2048, 64, 64], P(('leaf', 'sub')), may hold values from -0.75 to 0.75
- couplings: float32 [16384, 64, 64], P(('leaf', 'sub')), may hold values from -0.25 to 0.25
- top_coupling: float32 [128, 128, 64, 64], P('leaf', None, 'sub'), may hold values from -0.25 to 0.25
- send_leaf: int32 [128, 4, 128, 1], P('leaf', 'sub'), may hold values from 0 to 3
- list_slot: int32 [2048, 8], P(('leaf', 'sub')), may hold values from 0 to 127, as said below
- list_block: int32 [2048, 8], P(('leaf', 'sub')), may hold values from 0 to 31
Outputs:
- result: float32 [64, 524288], P(None, ('leaf', 'sub'))
The draws below stay inside these ranges and needn't reach their ends.
Inputs may be any that keep to these rules, and one draw needn't show every extreme that they name: send_leaf[e, s, d, c] is the leaf, among the 4 of device (e, s), whose skeleton fills slot c of what that device sends to device (d, s). `list_slot`: a list entry q names slot q % 1 from the device q // 1 of the leaf axis with the same sub index; where a device's 4 * 8 list entries are at least 128, every slot is named by some entry of that device, else the device's entries are all different. `list_block`: a list entry names one of the 32 coupling blocks of the leaf's own device.
All inputs are finite; a program needn't handle non-finite values.
Results may differ from the reference program's by a relative error of at most 0.0001.
Values sent between devices are 32-bit elements; how exact they have to be, the bound alone decides.
A program may use at most 64 MiB of HBM per device.

```python
import math
import jax
import jax.numpy as jnp
from jax import lax

LEAF = 256
R = 64
NRHS = 64
LEAVES_LOC = 4
K = 8
CAP = 1
NB = 32
NLEAVES = 2048
NPTS = 524288
N_LEAF = 128
N_SUB = 4


def draw_list_slot(key, part):
    slot_count = N_LEAF * CAP
    reads = LEAVES_LOC * K
    device_count = NLEAVES // LEAVES_LOC

    def one_device(index):
        device_key = jax.random.fold_in(jax.random.fold_in(key, 7919), index)
        slots = jax.random.permutation(jax.random.fold_in(device_key, 1), slot_count).astype(jnp.int32)
        order = jax.random.permutation(jax.random.fold_in(device_key, 2), reads).astype(jnp.int32)
        return slots[order % slot_count]
    values = jax.vmap(one_device)(jnp.arange(device_count, dtype=jnp.int32))
    return values.reshape(NLEAVES, K).astype(jnp.int32)


def set_ends(values, own_key, low, high):
    spot = [jax.random.randint(jax.random.fold_in(own_key, axis), (), 0, length) for axis, length in enumerate(values.shape)]
    main_axis = values.shape.index(max(values.shape))
    next_to = spot[:main_axis] + [(spot[main_axis] + 1) % values.shape[main_axis]] + spot[main_axis + 1:]
    return values.at[tuple(spot)].set(low).at[tuple(next_to)].set(high)


def spiked(array, stream_key, source, target, shards_of, factor):
    def block_of(dim):
        return (jnp.arange(array.shape[dim]) // (array.shape[dim] // shards_of)).reshape((-1,) + (1,) * (array.ndim - 1 - dim))

    first = jax.random.permutation(stream_key, shards_of)[block_of(target)]
    second = (block_of(target) + shards_of // 2) % shards_of
    return jnp.where((block_of(source) == first) | (block_of(source) == second), factor * array, array)


def block_scale(own_key, dims, split, low, largest):
    def one(position, shards_of):
        steps = jax.random.uniform(jax.random.fold_in(jax.random.fold_in(own_key, 6), position), (shards_of,), jnp.float32, low / len(split), largest / len(split))
        return jnp.repeat(jnp.exp(steps), dims[position] // shards_of).reshape((-1,) + (1,) * (len(dims) - position - 1))

    level = one(*split[0])
    for cut in split[1:]:
        level = level * one(*cut)
    return level


def centred(key, shape, deviation, bound, pieces=(), kind=jnp.bfloat16):
    values = jax.random.normal(key, shape, jnp.float32) * deviation
    if len(pieces) > 0:
        values = block_scale(key, shape, pieces, -0.22, 0.18) * values
    return jnp.clip(values, min=-bound, max=bound).astype(kind)


def heavy_noise(rng, extent, spread, reach, cuts, heavy, kind=jnp.bfloat16):
    drawn = spread * jax.random.normal(rng, extent, jnp.float32)
    if cuts:
        drawn = drawn * block_scale(rng, extent, cuts, -0.22, 0.18)
    return jnp.clip(spiked(drawn, jax.random.fold_in(rng, 3), *heavy), -reach, reach).astype(kind)


def setup_inputs(seed: int = 0) -> dict:
    seeds = jax.random.split(jax.random.key(seed), 11)
    field = centred(seeds[0], (NRHS, NPTS), 1.0, 6.0, ((1, 512),), jnp.float32)
    coords = centred(seeds[1], (3, NPTS), 1.0, 6.0, ((1, 512),), jnp.float32)
    basis = centred(seeds[2], (NLEAVES, R, LEAF), LEAF ** -0.5, 0.375, ((0, 512),), jnp.float32)
    up_transfer = centred(seeds[3], (NLEAVES, R, R), (R * LEAVES_LOC * N_SUB) ** -0.5, 0.1875, ((0, 512),), jnp.float32)
    down_transfer = centred(seeds[4], (NLEAVES, R, R), R ** -0.5, 0.75, ((0, 512),), jnp.float32)
    couplings = centred(seeds[5], (NB * N_LEAF * N_SUB, R, R), (R * K) ** -0.5, 0.25, ((0, 512),), jnp.float32)
    top_coupling = heavy_noise(seeds[6], (N_LEAF, N_LEAF, R, R), (R * N_LEAF) ** -0.5, 0.25, ((0, 128), (2, 4)), (1, 0, 128, 5.5), jnp.float32)
    send_leaf = set_ends(jax.random.randint(seeds[7], (N_LEAF, N_SUB, N_LEAF, CAP), 0, LEAVES_LOC), jax.random.fold_in(seeds[7], 1), 0, LEAVES_LOC - 1).astype(jnp.int32)
    list_slot = draw_list_slot(jax.random.fold_in(seeds[10], 71), 0)
    list_block = set_ends(jax.random.randint(seeds[9], (NLEAVES, K), 0, NB), jax.random.fold_in(seeds[9], 1), 0, NB - 1).astype(jnp.int32)
    return {"field": field, "coords": coords, "basis": basis, "up_transfer": up_transfer, "down_transfer": down_transfer, "couplings": couplings, "top_coupling": top_coupling, "send_leaf": send_leaf, "list_slot": list_slot, "list_block": list_block}


highest = lax.Precision.HIGHEST

def kernel_block(source_points, target_points):
    dist = jnp.zeros((source_points.shape[1], target_points.shape[1]), jnp.float32)
    for component in range(3):
        gap = source_points[component][:, None] - target_points[component][None, :]
        dist = dist + gap * gap
    return jnp.exp(-0.5 * dist) * (1.0 / math.sqrt(LEAF))

def one_product(field, coords, basis, up_transfer, down_transfer, couplings, top_coupling, send_leaf, list_slot, list_block):
    leaf_field = field.reshape(NRHS, NLEAVES, LEAF).transpose(1, 0, 2)
    leaf_coords = coords.reshape(3, NLEAVES, LEAF).transpose(1, 0, 2)
    zero_field = jnp.zeros((1, NRHS, LEAF), jnp.float32)
    zero_coords = jnp.zeros((1, 3, LEAF), jnp.float32)
    pad_field = jnp.concatenate([zero_field, leaf_field, zero_field], 0)
    pad_coords = jnp.concatenate([zero_coords, leaf_coords, zero_coords], 0)

    def near_block(block_index):
        first = block_index * LEAVES_LOC + jnp.arange(LEAVES_LOC, dtype=jnp.int32)
        window_field = jnp.concatenate([pad_field[first], pad_field[first + 1], pad_field[first + 2]], 2)
        window_coords = jnp.concatenate([pad_coords[first], pad_coords[first + 1], pad_coords[first + 2]], 2)
        own_coords = pad_coords[first + 1]
        kernels = jax.vmap(kernel_block)(window_coords, own_coords)
        return jnp.einsum('lpb,lba->lpa', window_field, kernels, precision=highest)
    near = lax.map(near_block, jnp.arange(NLEAVES // LEAVES_LOC, dtype=jnp.int32)).reshape(NLEAVES, NRHS, LEAF)
    skeleton = jnp.einsum('lpa,lra->lpr', leaf_field, basis, precision=highest)
    leaf_ids = jnp.arange(NLEAVES, dtype=jnp.int32)
    device = leaf_ids // LEAVES_LOC
    dest_leaf = device // N_SUB
    dest_sub = device % N_SUB
    peer = list_slot // CAP
    slot = list_slot % CAP
    source = (peer * N_SUB + dest_sub[:, None]) * LEAVES_LOC + send_leaf[peer, dest_sub[:, None], dest_leaf[:, None], slot]
    block = device[:, None] * NB + list_block
    far = jnp.zeros((NLEAVES, NRHS, R), jnp.float32)
    for entry in range(K):
        far = far + jnp.einsum('lpr,lrq->lpq', skeleton[source[:, entry]], couplings[block[:, entry]], precision=highest)
    parent = jnp.einsum('lpr,lrq->lpq', skeleton, up_transfer, precision=highest)
    parent = parent.reshape(N_LEAF, LEAVES_LOC * N_SUB, NRHS, R).sum(1)
    top_term = jnp.einsum('epr,derq->dpq', parent, top_coupling, precision=highest)
    top_leaf = jnp.repeat(top_term, LEAVES_LOC * N_SUB, axis=0)
    coef = far + jnp.einsum('lpr,lrq->lpq', top_leaf, down_transfer, precision=highest)
    total = near + jnp.einsum('lpr,lra->lpa', coef, basis, precision=highest)
    return total.transpose(1, 0, 2).reshape(NRHS, NPTS)

def reference(field, coords, basis, up_transfer, down_transfer, couplings, top_coupling, send_leaf, list_slot, list_block):
    first_pass = one_product(field, coords, basis, up_transfer, down_transfer, couplings, top_coupling, send_leaf, list_slot, list_block)
    return one_product(first_pass, coords, basis, up_transfer, down_transfer, couplings, top_coupling, send_leaf, list_slot, list_block)
```

```python
import math

import jax
import jax.numpy as jnp
from jax import lax
from jax.sharding import PartitionSpec as P

precise = lax.Precision.HIGH


def halo(block, axes, count):
    forward = [(i, i + 1) for i in range(count - 1)]
    backward = [(target, source) for source, target in forward]
    low = lax.ppermute(block[:, -1], axes, forward)
    high = lax.ppermute(block[:, 0], axes, backward)
    return jnp.concatenate([low[:, None], block, high[:, None]], axis=1)


def shifted(values, axis, count, step):
    return lax.ppermute(values, axis, [(i, (i + step) % count) for i in range(count)])


def kernel_blocks(sources, targets, leaf_size):
    dist = 0.0
    for component in range(3):
        gap = sources[component][:, :, None] - targets[component][:, None, :]
        dist = dist + gap * gap
    return jnp.exp(-0.5 * dist) * (1.0 / math.sqrt(leaf_size))


def fold(values):
    half = values.shape[-2] // 2
    return jnp.concatenate([values[..., :half, :], values[..., half:, :]], axis=-1)


def unfold(values):
    half = values.shape[-1] // 2
    return jnp.concatenate([values[..., :half], values[..., half:]], axis=-2)


def one_product(field, near_kernels, basis, up, down, couplings, top, send, slots, blocks):
    rhs, leaves, size = field.shape
    rank = basis.shape[1]
    subs = lax.axis_size("sub")
    quarter = rank // subs
    sub = lax.axis_index("sub")
    count = lax.axis_size("leaf") * subs
    skeleton = jnp.einsum("pla,lra->lpr", field, basis, precision=precise)
    parent_t = jnp.einsum("lpr,lrq->qp", skeleton, up, precision=precise)
    parts = parent_t.reshape(subs, quarter, rhs)
    own = lax.dynamic_index_in_dim(parts, sub, 0, keepdims=False)
    for step in range(1, subs):
        piece = lax.dynamic_index_in_dim(parts, (sub + step) % subs, 0, keepdims=False)
        own = own + shifted(piece, "sub", subs, step)
    packed = fold(skeleton)[send]
    rows = packed.shape[1]
    parent = jnp.broadcast_to(fold(own)[None], (packed.shape[0], quarter // 2, 2 * rhs))
    outgoing = jnp.concatenate([packed, parent], axis=1)
    incoming = lax.all_to_all(outgoing, "leaf", split_axis=0, concat_axis=0, tiled=True)
    padded = halo(field, ("leaf", "sub"), count)
    near = 0.0
    for side in range(3):
        near = near + jnp.einsum(
            "plb,lba->pla", padded[:, side : side + leaves], near_kernels[side], precision=precise
        )
    parents = unfold(incoming[:, rows:])
    top_part = jnp.einsum("erp,erq->pq", parents, top, precision=precise)
    folded = fold(top_part)
    summed = folded
    for step in range(1, subs):
        summed = summed + shifted(folded, "sub", subs, step)
    top_term = unfold(summed)
    gathered = unfold(incoming[slots][:, :, :rows])
    far = jnp.einsum("lkpr,lkrq->lpq", gathered, couplings[blocks], precision=precise)
    coef = far + jnp.einsum("pr,lrq->lpq", top_term, down, precision=precise)
    return near + jnp.einsum("lpr,lra->pla", coef, basis, precision=precise)


def local(
    field, coords, basis, up_transfer, down_transfer, couplings, top_coupling, send_leaf, list_slot, list_block
):
    rhs = field.shape[0]
    leaves, _, size = basis.shape
    count = lax.axis_size("leaf") * lax.axis_size("sub")
    points = coords.reshape(3, leaves, size)
    all_points = halo(points, ("leaf", "sub"), count)
    near_kernels = [
        kernel_blocks(all_points[:, side : side + leaves], points, size) for side in range(3)
    ]
    current = field.reshape(rhs, leaves, size)
    for repeat in range(2):
        current = one_product(
            current,
            near_kernels,
            basis,
            up_transfer,
            down_transfer,
            couplings,
            top_coupling[0],
            send_leaf.reshape(-1),
            list_slot,
            list_block,
        )
    return current.reshape(rhs, leaves * size)


def solution(mesh):
    joined = ("leaf", "sub")
    in_specs = (
        P(None, joined),
        P(None, joined),
        P(joined, None, None),
        P(joined, None, None),
        P(joined, None, None),
        P(joined, None, None),
        P("leaf", None, "sub", None),
        P("leaf", "sub", None, None),
        P(joined, None),
        P(joined, None),
    )
    return jax.shard_map(local, mesh=mesh, in_specs=in_specs, out_specs=P(None, joined), check_vma=False)
```

```python
import functools
import math

import jax
import jax.numpy as jnp
from jax import lax
from jax.experimental import pallas as pl
from jax.experimental.pallas import tpu as pltpu
from jax.sharding import PartitionSpec as P

precise = lax.Precision.HIGH
MESH = pl.DeviceIdType.MESH
SIDE = 8
CORES = 2


def halo(block, axes, count):
    forward = [(i, i + 1) for i in range(count - 1)]
    backward = [(target, source) for source, target in forward]
    low = lax.ppermute(block[:, -1], axes, forward)
    high = lax.ppermute(block[:, 0], axes, backward)
    return jnp.concatenate([low[:, None], block, high[:, None]], axis=1)


def kernel_blocks(sources, targets, leaf_size):
    dist = 0.0
    for component in range(3):
        gap = sources[component][:, :, None] - targets[component][:, None, :]
        dist = dist + gap * gap
    return jnp.exp(-0.5 * dist) * (1.0 / math.sqrt(leaf_size))


def fold(values):
    half = values.shape[-2] // 2
    return jnp.concatenate([values[..., :half, :], values[..., half:, :]], axis=-1)


def unfold(values):
    half = values.shape[-1] // 2
    return jnp.concatenate([values[..., :half], values[..., half:]], axis=-2)


def ring_events():
    events = []
    reach = SIDE // 2
    for a in range(-reach, reach):
        plus, minus = (reach, reach - 1) if a % 2 == 0 else (reach - 1, reach)
        for b in range(-plus, minus + 1):
            events.append((abs(a) + abs(b), abs(b), a, b, plus, minus))
    return sorted(events)


def place():
    leaf = lax.axis_index("leaf")
    return leaf // (SIDE * CORES), (leaf // CORES) % SIDE, leaf % CORES, lax.axis_index("sub")


def leaf_of(y, z, core):
    return (y * SIDE + z) * CORES + core


def wrapped(index, step, size):
    return lax.rem(index + (step + size), size)


def exchange_kernel(
    subs,
    leaf_total,
    skeleton_ref,
    row_ref,
    parts_ref,
    edges_ref,
    gather_ref,
    halo_ref,
    sums_ref,
    ring_send,
    ring_recv,
    pair_send,
    pair_recv,
    small_send,
    small_recv,
):
    y, z, core, sub = place()
    leaf = lax.axis_index("leaf")
    rank = skeleton_ref.shape[1]
    partner = (leaf_of(y, z, 1 - core), sub)
    y_up = (leaf_of(wrapped(y, 1, SIDE), z, core), sub)
    y_down = (leaf_of(wrapped(y, -1, SIDE), z, core), sub)
    z_up = (leaf_of(y, wrapped(z, 1, SIDE), core), sub)
    z_down = (leaf_of(y, wrapped(z, -1, SIDE), core), sub)
    peers = [(leaf, wrapped(sub, step, subs)) for step in range(1, subs)]
    position = leaf * subs + sub
    total = leaf_total * subs
    after = wrapped(position, 1, total)
    before = wrapped(position, -1, total)
    after = (after // subs, after % subs)
    before = (before // subs, before % subs)

    barrier = pltpu.get_barrier_semaphore()
    others = [partner, y_up, y_down, z_up, z_down] + peers + [after, before]
    for other in others:
        pl.semaphore_signal(barrier, inc=1, device_id=other, device_id_type=MESH)

    gather_ref[0, y, z, core, :rank] = skeleton_ref[0]
    gather_ref[1, y, z, core, :rank] = skeleton_ref[1]
    gather_ref[1, y, z, core, rank:] = row_ref[...]
    pl.semaphore_wait(barrier, len(others))

    small = []
    for step, peer in enumerate(peers):
        small.append(
            pltpu.make_async_remote_copy(
                src_ref=parts_ref.at[peer[1]],
                dst_ref=sums_ref.at[step],
                send_sem=small_send.at[step],
                recv_sem=small_recv.at[step],
                device_id=peer,
                device_id_type=MESH,
            )
        )
    for way, other in enumerate((before, after)):
        small.append(
            pltpu.make_async_remote_copy(
                src_ref=edges_ref.at[way],
                dst_ref=halo_ref.at[1 - way],
                send_sem=small_send.at[subs - 1 + way],
                recv_sem=small_recv.at[subs - 1 + way],
                device_id=other,
                device_id_type=MESH,
            )
        )
    for copy in small:
        copy.start()

    def block(half, a, b):
        if half == 0:
            return gather_ref.at[0, wrapped(y, b, SIDE), wrapped(z, a, SIDE), core]
        return gather_ref.at[1, wrapped(y, a, SIDE), wrapped(z, b, SIDE), core]

    first = ((z_up, z_down), (y_up, y_down))
    second = ((y_up, y_down), (z_up, z_down))

    def ring_copy(half, a, b, landed_a, landed_b, other):
        i, j = landed_a % SIDE, landed_b % SIDE
        here = block(half, a, b)
        return pltpu.make_async_remote_copy(
            src_ref=here,
            dst_ref=here,
            send_sem=ring_send.at[half, i, j],
            recv_sem=ring_recv.at[half, i, j],
            device_id=other,
            device_id_type=MESH,
        )

    def pair_copy(half, a, b):
        here = block(half, a, b)
        return pltpu.make_async_remote_copy(
            src_ref=here,
            dst_ref=here,
            send_sem=pair_send.at[half, a % SIDE, b % SIDE],
            recv_sem=pair_recv.at[half, a % SIDE, b % SIDE],
            device_id=partner,
            device_id_type=MESH,
        )

    sent = []

    def pass_on(half, a, b, plus, minus):
        copies = []
        up, down = first[half]
        reach = SIDE // 2
        if b == 0:
            if -reach < a <= 0:
                copies.append(ring_copy(half, a, b, a - 1, b, up))
            if 0 <= a < reach - 1:
                copies.append(ring_copy(half, a, b, a + 1, b, down))
        up, down = second[half]
        if -plus < b <= 0:
            copies.append(ring_copy(half, a, b, a, b - 1, up))
        if 0 <= b < minus:
            copies.append(ring_copy(half, a, b, a, b + 1, down))
        copies.append(pair_copy(half, a, b))
        for copy in copies:
            copy.start()
        sent.extend(copies)

    events = ring_events()
    _, _, a, b, plus, minus = events[0]
    pass_on(1, a, b, plus, minus)
    for copy in small[: subs - 1]:
        copy.wait_recv()
    parent = parts_ref[sub]
    for step in range(subs - 1):
        parent = parent + sums_ref[step]
    gather_ref[0, y, z, core, rank:] = parent
    pass_on(0, a, b, plus, minus)
    for _, _, a, b, plus, minus in events[1:]:
        for half in (1, 0):
            ring_copy(half, a, b, a, b, partner).wait_recv()
            pass_on(half, a, b, plus, minus)
    for copy in small:
        copy.wait_send()
    for copy in small[subs - 1 :]:
        copy.wait_recv()
    for copy in sent:
        copy.wait_send()
    for _, _, a, b, _, _ in events:
        for half in (0, 1):
            pair_copy(half, a, b).wait_recv()


def exchange(skeleton, row, parts, edges, subs, leaf_total):
    rows = skeleton.shape[1] + row.shape[0]
    lanes = skeleton.shape[2]
    vmem = pl.BlockSpec(memory_space=pltpu.VMEM)
    dma = pltpu.SemaphoreType.DMA
    return pl.pallas_call(
        functools.partial(exchange_kernel, subs, leaf_total),
        out_shape=(
            jax.ShapeDtypeStruct((2, SIDE, SIDE, CORES, rows, lanes), jnp.float32),
            jax.ShapeDtypeStruct(edges.shape, jnp.float32),
        ),
        in_specs=[vmem] * 4,
        out_specs=(vmem, vmem),
        scratch_shapes=[
            pltpu.VMEM((subs - 1,) + parts.shape[1:], jnp.float32),
            dma((2, SIDE, SIDE)),
            dma((2, SIDE, SIDE)),
            dma((2, SIDE, SIDE)),
            dma((2, SIDE, SIDE)),
            dma((subs + 1,)),
            dma((subs + 1,)),
        ],
        compiler_params=pltpu.CompilerParams(collective_id=0, has_side_effects=True),
        name="exchange",
    )(skeleton, row, parts, edges)


def sum_kernel(subs, in_ref, out_ref, sums_ref, send_sem, recv_sem):
    leaf, sub = lax.axis_index("leaf"), lax.axis_index("sub")
    peers = [(leaf, wrapped(sub, step, subs)) for step in range(1, subs)]
    barrier = pltpu.get_barrier_semaphore()
    for peer in peers:
        pl.semaphore_signal(barrier, inc=1, device_id=peer, device_id_type=MESH)
    pl.semaphore_wait(barrier, subs - 1)
    copies = [
        pltpu.make_async_remote_copy(
            src_ref=in_ref,
            dst_ref=sums_ref.at[step],
            send_sem=send_sem.at[step],
            recv_sem=recv_sem.at[step],
            device_id=peer,
            device_id_type=MESH,
        )
        for step, peer in enumerate(peers)
    ]
    for copy in copies:
        copy.start()
    result = in_ref[...]
    for step, copy in enumerate(copies):
        copy.wait_recv()
        result = result + sums_ref[step]
    out_ref[...] = result
    for copy in copies:
        copy.wait_send()


def sum_over_sub(values, subs):
    vmem = pl.BlockSpec(memory_space=pltpu.VMEM)
    dma = pltpu.SemaphoreType.DMA
    return pl.pallas_call(
        functools.partial(sum_kernel, subs),
        out_shape=jax.ShapeDtypeStruct(values.shape, jnp.float32),
        in_specs=[vmem],
        out_specs=vmem,
        scratch_shapes=[
            pltpu.VMEM((subs - 1,) + values.shape, jnp.float32),
            dma((subs - 1,)),
            dma((subs - 1,)),
        ],
        compiler_params=pltpu.CompilerParams(collective_id=1, has_side_effects=True),
        name="sum_over_sub",
    )(values)


def one_product(field, near_kernels, basis, up, down, couplings, top, row, slots, blocks):
    rhs, leaves, size = field.shape
    rank = basis.shape[1]
    subs = lax.axis_size("sub")
    leaf_total = lax.axis_size("leaf")
    leaf = lax.axis_index("leaf")
    skeleton = jnp.einsum("pla,lra->lpr", field, basis, precision=precise)
    parent_t = jnp.einsum("lpr,lrq->qp", skeleton, up, precision=precise)
    parts = fold(parent_t.reshape(subs, rank // subs, rhs))
    pairs = jnp.concatenate([skeleton[0::2], skeleton[1::2]], axis=-1)
    edges = jnp.stack([field[:, 0], field[:, -1]])
    gathered, sides = exchange(pairs, row, parts, edges, subs, leaf_total)
    gathered = gathered.reshape(2, leaf_total, -1, 2 * rank)
    parents = unfold(gathered[0, :, rhs:])
    top_part = jnp.einsum("erp,erq->pq", parents, top, precision=precise)
    top_term = unfold(sum_over_sub(fold(top_part), subs))
    padded = jnp.concatenate([sides[0][:, None], field, sides[1][:, None]], axis=1)
    near = 0.0
    for side in range(3):
        near = near + jnp.einsum(
            "plb,lba->pla", padded[:, side : side + leaves], near_kernels[side], precision=precise
        )
    chosen = lax.dynamic_index_in_dim(gathered[1, :, rhs], leaf, 1, keepdims=False)[slots]
    chosen = chosen.astype(jnp.int32)
    both = gathered[chosen // 2, slots, :rhs]
    source = jnp.where((chosen % 2 == 0)[..., None, None], both[..., :rank], both[..., rank:])
    far = jnp.einsum("lkpr,lkrq->lpq", source, couplings[blocks], precision=precise)
    coef = far + jnp.einsum("pr,lrq->lpq", top_term, down, precision=precise)
    return near + jnp.einsum("lpr,lra->pla", coef, basis, precision=precise)


def local(
    field, coords, basis, up_transfer, down_transfer, couplings, top_coupling, send_leaf, list_slot, list_block
):
    rhs = field.shape[0]
    leaves, _, size = basis.shape
    subs = lax.axis_size("sub")
    count = lax.axis_size("leaf") * subs
    position = lax.axis_index("leaf") * subs + lax.axis_index("sub")
    points = coords.reshape(3, leaves, size)
    all_points = halo(points, ("leaf", "sub"), count)
    near_kernels = []
    for side in range(3):
        index = position * leaves + jnp.arange(leaves) + (side - 1)
        present = (index >= 0) & (index < count * leaves)
        values = kernel_blocks(all_points[:, side : side + leaves], points, size)
        near_kernels.append(jnp.where(present[:, None, None], values, 0.0))
    row = jnp.broadcast_to(send_leaf.reshape(1, -1).astype(jnp.float32), (8, send_leaf.size))
    current = field.reshape(rhs, leaves, size)
    for repeat in range(2):
        current = one_product(
            current,
            near_kernels,
            basis,
            up_transfer,
            down_transfer,
            couplings,
            top_coupling[0],
            row,
            list_slot,
            list_block,
        )
    return current.reshape(rhs, leaves * size)


def solution(mesh):
    joined = ("leaf", "sub")
    in_specs = (
        P(None, joined),
        P(None, joined),
        P(joined, None, None),
        P(joined, None, None),
        P(joined, None, None),
        P(joined, None, None),
        P("leaf", None, "sub", None),
        P("leaf", "sub", None, None),
        P(joined, None),
        P(joined, None),
    )
    return jax.shard_map(local, mesh=mesh, in_specs=in_specs, out_specs=P(None, joined), check_vma=False)
```

```python
import functools
import math

import jax
import jax.numpy as jnp
from jax import lax
from jax.experimental import pallas as pl
from jax.experimental.pallas import tpu as pltpu
from jax.sharding import PartitionSpec as P

precise = lax.Precision.HIGH
MESH = pl.DeviceIdType.MESH
SIDE = 8
CORES = 2


def halo(block, axes, count):
    forward = [(i, i + 1) for i in range(count - 1)]
    backward = [(target, source) for source, target in forward]
    low = lax.ppermute(block[:, -1], axes, forward)
    high = lax.ppermute(block[:, 0], axes, backward)
    return jnp.concatenate([low[:, None], block, high[:, None]], axis=1)


def kernel_blocks(sources, targets, leaf_size):
    dist = 0.0
    for component in range(3):
        gap = sources[component][:, :, None] - targets[component][:, None, :]
        dist = dist + gap * gap
    return jnp.exp(-0.5 * dist) * (1.0 / math.sqrt(leaf_size))


def fold(values):
    half = values.shape[-2] // 2
    return jnp.concatenate([values[..., :half, :], values[..., half:, :]], axis=-1)


def unfold(values):
    half = values.shape[-1] // 2
    return jnp.concatenate([values[..., :half], values[..., half:]], axis=-2)


def place():
    leaf = lax.axis_index("leaf")
    return leaf // (SIDE * CORES), (leaf // CORES) % SIDE, leaf % CORES, lax.axis_index("sub")


def leaf_of(y, z, core):
    return (y * SIDE + z) * CORES + core


def wrapped(index, step, size):
    return lax.rem(index + (step + size), size)


def exchange_kernel(
    subs,
    leaf_total,
    skeleton_ref,
    row_ref,
    parts_ref,
    edges_ref,
    where_ref,
    source_ref,
    parents_ref,
    halo_ref,
    gather_ref,
    sums_ref,
    near_send,
    near_recv,
    slab_send,
    slab_recv,
    pair_send,
    pair_recv,
    small_send,
    small_recv,
):
    y, z, core, sub = place()
    leaf = lax.axis_index("leaf")
    rank = skeleton_ref.shape[1]
    reach = SIDE // 2
    width = SIDE // 2
    partner = (leaf_of(y, z, 1 - core), sub)
    y_ring = (
        (leaf_of(wrapped(y, 1, SIDE), z, core), sub),
        (leaf_of(wrapped(y, -1, SIDE), z, core), sub),
    )
    z_ring = (
        (leaf_of(y, wrapped(z, 1, SIDE), core), sub),
        (leaf_of(y, wrapped(z, -1, SIDE), core), sub),
    )
    peers = [(leaf, wrapped(sub, step, subs)) for step in range(1, subs)]
    position = leaf * subs + sub
    total = leaf_total * subs
    after = wrapped(position, 1, total)
    before = wrapped(position, -1, total)
    after = (after // subs, after % subs)
    before = (before // subs, before % subs)

    barrier = pltpu.get_barrier_semaphore()
    others = [partner, *y_ring, *z_ring] + peers + [after, before]
    for other in others:
        pl.semaphore_signal(barrier, inc=1, device_id=other, device_id_type=MESH)

    inner, outer = (z, y), (y, z)
    inner_ring, outer_ring = (z_ring, y_ring), (y_ring, z_ring)

    def slot(half, a, b):
        return (core * SIDE + wrapped(outer[half], b, SIDE)) * SIDE + wrapped(inner[half], a, SIDE)

    own = (slot(0, 0, 0), slot(1, 0, 0))
    gather_ref[0, own[0], :rank] = skeleton_ref[0]
    gather_ref[1, own[1], :rank] = skeleton_ref[1]
    gather_ref[1, own[1], rank:] = row_ref[...]
    pl.semaphore_wait(barrier, len(others))

    small = []
    for step, peer in enumerate(peers):
        small.append(
            pltpu.make_async_remote_copy(
                src_ref=parts_ref.at[peer[1]],
                dst_ref=sums_ref.at[step],
                send_sem=small_send.at[step],
                recv_sem=small_recv.at[step],
                device_id=peer,
                device_id_type=MESH,
            )
        )
    for way, other in enumerate((before, after)):
        small.append(
            pltpu.make_async_remote_copy(
                src_ref=edges_ref.at[way],
                dst_ref=halo_ref.at[1 - way],
                send_sem=small_send.at[subs - 1 + way],
                recv_sem=small_recv.at[subs - 1 + way],
                device_id=other,
                device_id_type=MESH,
            )
        )
    for copy in small[: subs - 1]:
        copy.start()

    sent = []

    def near_copy(half, a, way):
        here = gather_ref.at[half, slot(half, a, 0)]
        landed = (a - 1 if way == 0 else a + 1) % SIDE
        return pltpu.make_async_remote_copy(
            src_ref=here,
            dst_ref=here,
            send_sem=near_send.at[half, landed],
            recv_sem=near_recv.at[half, landed],
            device_id=inner_ring[half][way],
            device_id_type=MESH,
        )

    def slab(half, group, b):
        first = (core * SIDE + wrapped(outer[half], b, SIDE)) * SIDE + group * width
        return gather_ref.at[half, pl.ds(first, width)]

    def slab_copy(half, group, b, way):
        here = slab(half, group, b)
        landed = (b - 1 if way == 0 else b + 1) % SIDE
        return pltpu.make_async_remote_copy(
            src_ref=here,
            dst_ref=here,
            send_sem=slab_send.at[half, group, landed],
            recv_sem=slab_recv.at[half, group, landed],
            device_id=outer_ring[half][way],
            device_id_type=MESH,
        )

    def pair_copy(half, group, b):
        here = slab(half, group, b)
        return pltpu.make_async_remote_copy(
            src_ref=here,
            dst_ref=here,
            send_sem=pair_send.at[half, group, b % SIDE],
            recv_sem=pair_recv.at[half, group, b % SIDE],
            device_id=partner,
            device_id_type=MESH,
        )

    def go(copy):
        copy.start()
        sent.append(copy)

    for way in (0, 1):
        go(near_copy(1, 0, way))
    for copy in small[: subs - 1]:
        copy.wait_recv()
    parent = parts_ref[sub]
    for step in range(subs - 1):
        parent = parent + sums_ref[step]
    gather_ref[0, own[0], rank:] = parent
    for copy in small[subs - 1 :]:
        copy.start()
    for way in (0, 1):
        go(near_copy(0, 0, way))

    def limit(group, way):
        return reach if group == way else reach - 1

    for step in range(1, reach + 1):
        for half in (1, 0):
            for way in (0, 1):
                if step <= reach - way:
                    a = -step if way == 0 else step
                    near_copy(half, a + 1 if way == 0 else a - 1, way).wait_recv()
                    if step < reach - way:
                        go(near_copy(half, a, way))
            if step == reach:
                for way in (0, 1):
                    for group in (way, 1 - way):
                        go(slab_copy(half, group, 0, way))
                for group in (0, 1):
                    go(pair_copy(half, group, 0))
    for step in range(1, reach + 1):
        for half in (1, 0):
            for turn in (0, 1):
                for way in (0, 1):
                    group = way if turn == 0 else 1 - way
                    if step > limit(group, way):
                        continue
                    b = -step if way == 0 else step
                    slab_copy(half, group, b + 1 if way == 0 else b - 1, way).wait_recv()
                    if step < limit(group, way):
                        go(slab_copy(half, group, b, way))
                    go(pair_copy(half, group, b))
    for copy in small:
        copy.wait_send()
    for copy in small[subs - 1 :]:
        copy.wait_recv()
    for half in (1, 0):
        for group in (0, 1):
            for b in range(SIDE):
                pair_copy(half, group, b).wait_recv()

    plane = SIDE * SIDE
    for side in range(CORES):
        parents_ref[:, side] = gather_ref[0, side * plane : (side + 1) * plane, rank:]
    leaves, entries = source_ref.shape[0], source_ref.shape[2] // rank
    lane = lax.broadcasted_iota(jnp.int32, (rank, row_ref.shape[1]), 1)
    for target in range(leaves):
        for entry in range(entries):
            at_0 = where_ref[0, target * entries + entry]
            at_1 = where_ref[1, target * entries + entry]
            low = gather_ref[0, at_0, :rank]
            high = gather_ref[1, at_1, :rank]
            named = jnp.broadcast_to(gather_ref[1, at_1, rank : rank + 1], lane.shape)
            named = jnp.sum(jnp.where(lane == leaf, named, 0.0), axis=1, keepdims=True)
            both = jnp.where(named < 1.5, low, high)
            odd = (named == 1.0) | (named == 3.0)
            source_ref[target, :, entry * rank : (entry + 1) * rank] = jnp.where(
                odd, both[:, rank:], both[:, :rank]
            )
    for copy in sent:
        copy.wait_send()


def exchange(skeleton, row, parts, edges, where, leaves, subs, leaf_total):
    rank = skeleton.shape[1]
    rows = rank + row.shape[0]
    lanes = skeleton.shape[2]
    entries = where.shape[1] // leaves
    vmem = pl.BlockSpec(memory_space=pltpu.VMEM)
    dma = pltpu.SemaphoreType.DMA
    return pl.pallas_call(
        functools.partial(exchange_kernel, subs, leaf_total),
        out_shape=(
            jax.ShapeDtypeStruct((leaves, rank, entries * rank), jnp.float32),
            jax.ShapeDtypeStruct((leaf_total // CORES, CORES, row.shape[0], lanes), jnp.float32),
            jax.ShapeDtypeStruct(edges.shape, jnp.float32),
        ),
        in_specs=[vmem] * 4 + [pl.BlockSpec(memory_space=pltpu.SMEM)],
        out_specs=(vmem, vmem, vmem),
        scratch_shapes=[
            pltpu.VMEM((2, leaf_total, rows, lanes), jnp.float32),
            pltpu.VMEM((subs - 1,) + parts.shape[1:], jnp.float32),
            dma((2, SIDE)),
            dma((2, SIDE)),
            dma((2, 2, SIDE)),
            dma((2, 2, SIDE)),
            dma((2, 2, SIDE)),
            dma((2, 2, SIDE)),
            dma((subs + 1,)),
            dma((subs + 1,)),
        ],
        compiler_params=pltpu.CompilerParams(collective_id=0, has_side_effects=True),
        name="exchange",
    )(skeleton, row, parts, edges, where)


def sum_kernel(subs, in_ref, out_ref, sums_ref, send_sem, recv_sem):
    leaf, sub = lax.axis_index("leaf"), lax.axis_index("sub")
    peers = [(leaf, wrapped(sub, step, subs)) for step in range(1, subs)]
    barrier = pltpu.get_barrier_semaphore()
    for peer in peers:
        pl.semaphore_signal(barrier, inc=1, device_id=peer, device_id_type=MESH)
    pl.semaphore_wait(barrier, subs - 1)
    copies = [
        pltpu.make_async_remote_copy(
            src_ref=in_ref,
            dst_ref=sums_ref.at[step],
            send_sem=send_sem.at[step],
            recv_sem=recv_sem.at[step],
            device_id=peer,
            device_id_type=MESH,
        )
        for step, peer in enumerate(peers)
    ]
    for copy in copies:
        copy.start()
    result = in_ref[...]
    for step, copy in enumerate(copies):
        copy.wait_recv()
        result = result + sums_ref[step]
    out_ref[...] = result
    for copy in copies:
        copy.wait_send()


def sum_over_sub(values, subs):
    vmem = pl.BlockSpec(memory_space=pltpu.VMEM)
    dma = pltpu.SemaphoreType.DMA
    return pl.pallas_call(
        functools.partial(sum_kernel, subs),
        out_shape=jax.ShapeDtypeStruct(values.shape, jnp.float32),
        in_specs=[vmem],
        out_specs=vmem,
        scratch_shapes=[
            pltpu.VMEM((subs - 1,) + values.shape, jnp.float32),
            dma((subs - 1,)),
            dma((subs - 1,)),
        ],
        compiler_params=pltpu.CompilerParams(collective_id=1, has_side_effects=True),
        name="sum_over_sub",
    )(values)


def one_product(field, near_kernels, basis, up, down, chosen, top, row, where):
    rhs, leaves, size = field.shape
    rank = basis.shape[1]
    subs = lax.axis_size("sub")
    leaf_total = lax.axis_size("leaf")
    skeleton = jnp.einsum("pla,lra->lpr", field, basis, precision=precise)
    parent_t = jnp.einsum("lpr,lrq->qp", skeleton, up, precision=precise)
    parts = fold(parent_t.reshape(subs, rank // subs, rhs))
    pairs = jnp.concatenate([skeleton[0::2], skeleton[1::2]], axis=-1)
    edges = jnp.stack([field[:, 0], field[:, -1]])
    sources, parents, sides = exchange(pairs, row, parts, edges, where, leaves, subs, leaf_total)
    parents = unfold(parents.reshape(leaf_total, -1, 2 * rank))
    top_part = jnp.einsum("erp,erq->pq", parents, top, precision=precise)
    top_term = unfold(sum_over_sub(fold(top_part), subs))
    padded = jnp.concatenate([sides[0][:, None], field, sides[1][:, None]], axis=1)
    near = 0.0
    for side in range(3):
        near = near + jnp.einsum(
            "plb,lba->pla", padded[:, side : side + leaves], near_kernels[side], precision=precise
        )
    far = jnp.einsum("lpm,lmq->lpq", sources, chosen, precision=precise)
    coef = far + jnp.einsum("pr,lrq->lpq", top_term, down, precision=precise)
    return near + jnp.einsum("lpr,lra->pla", coef, basis, precision=precise)


def local(
    field, coords, basis, up_transfer, down_transfer, couplings, top_coupling, send_leaf, list_slot, list_block
):
    rhs = field.shape[0]
    leaves, _, size = basis.shape
    subs = lax.axis_size("sub")
    count = lax.axis_size("leaf") * subs
    position = lax.axis_index("leaf") * subs + lax.axis_index("sub")
    points = coords.reshape(3, leaves, size)
    all_points = halo(points, ("leaf", "sub"), count)
    near_kernels = []
    for side in range(3):
        index = position * leaves + jnp.arange(leaves) + (side - 1)
        present = (index >= 0) & (index < count * leaves)
        values = kernel_blocks(all_points[:, side : side + leaves], points, size)
        near_kernels.append(jnp.where(present[:, None, None], values, 0.0))
    row = jnp.broadcast_to(send_leaf.reshape(1, -1).astype(jnp.float32), (8, send_leaf.size))
    rank = basis.shape[1]
    chosen = couplings[list_block].reshape(leaves, -1, rank)
    flat = list_slot.reshape(-1)
    slot_y, slot_z, slot_core = flat // (SIDE * CORES), (flat // CORES) % SIDE, flat % CORES
    where = jnp.stack(
        [(slot_core * SIDE + slot_y) * SIDE + slot_z, (slot_core * SIDE + slot_z) * SIDE + slot_y]
    )
    current = field.reshape(rhs, leaves, size)
    for repeat in range(2):
        current = one_product(
            current,
            near_kernels,
            basis,
            up_transfer,
            down_transfer,
            chosen,
            top_coupling[0],
            row,
            where,
        )
    return current.reshape(rhs, leaves * size)


def solution(mesh):
    joined = ("leaf", "sub")
    in_specs = (
        P(None, joined),
        P(None, joined),
        P(joined, None, None),
        P(joined, None, None),
        P(joined, None, None),
        P(joined, None, None),
        P("leaf", None, "sub", None),
        P("leaf", "sub", None, None),
        P(joined, None),
        P(joined, None),
    )
    return jax.shard_map(local, mesh=mesh, in_specs=in_specs, out_specs=P(None, joined), check_vma=False)
```

```python
import functools
import math

import jax
import jax.numpy as jnp
from jax import lax
from jax.experimental import pallas as pl
from jax.experimental.pallas import tpu as pltpu
from jax.sharding import PartitionSpec as P

precise = lax.Precision.HIGH
MESH = pl.DeviceIdType.MESH
SIDE = 8
CORES = 2


def kernel_blocks(sources, targets, leaf_size):
    dist = 0.0
    for component in range(3):
        gap = sources[component][:, :, None] - targets[component][:, None, :]
        dist = dist + gap * gap
    return jnp.exp(-0.5 * dist) * (1.0 / math.sqrt(leaf_size))


def fold(values):
    half = values.shape[-2] // 2
    return jnp.concatenate([values[..., :half, :], values[..., half:, :]], axis=-1)


def unfold(values):
    half = values.shape[-1] // 2
    return jnp.concatenate([values[..., :half], values[..., half:]], axis=-2)


def place():
    leaf = lax.axis_index("leaf")
    return leaf // (SIDE * CORES), (leaf // CORES) % SIDE, leaf % CORES, lax.axis_index("sub")


def leaf_of(y, z, core):
    return (y * SIDE + z) * CORES + core


def wrapped(index, step, size):
    return lax.rem(index + (step + size), size)


def exchange_kernel(
    subs,
    leaf_total,
    skeleton_ref,
    row_ref,
    parts_ref,
    edges_ref,
    where_ref,
    source_ref,
    parents_ref,
    halo_ref,
    gather_ref,
    sums_ref,
    near_send,
    near_recv,
    slab_send,
    slab_recv,
    pair_send,
    pair_recv,
    small_send,
    small_recv,
):
    y, z, core, sub = place()
    leaf = lax.axis_index("leaf")
    rank = skeleton_ref.shape[1]
    reach = SIDE // 2
    width = SIDE // 2
    partner = (leaf_of(y, z, 1 - core), sub)
    y_line = [(leaf_of(wrapped(y, step, SIDE), z, core), sub) for step in range(1, SIDE)]
    z_line = [(leaf_of(y, wrapped(z, step, SIDE), core), sub) for step in range(1, SIDE)]
    peers = [(leaf, wrapped(sub, step, subs)) for step in range(1, subs)]
    position = leaf * subs + sub
    total = leaf_total * subs
    after = wrapped(position, 1, total)
    before = wrapped(position, -1, total)
    after = (after // subs, after % subs)
    before = (before // subs, before % subs)

    barrier = pltpu.get_barrier_semaphore()
    others = [partner] + y_line + z_line + peers + [after, before]
    for other in others:
        pl.semaphore_signal(barrier, inc=1, device_id=other, device_id_type=MESH)

    inner, outer = (z, y), (y, z)
    inner_line = (z_line, y_line)
    outer_ring = ((y_line[0], y_line[-1]), (z_line[0], z_line[-1]))

    def slot(half, a, b):
        return (core * SIDE + wrapped(outer[half], b, SIDE)) * SIDE + wrapped(inner[half], a, SIDE)

    own = (slot(0, 0, 0), slot(1, 0, 0))
    gather_ref[0, own[0], :rank] = skeleton_ref[0]
    gather_ref[1, own[1], :rank] = skeleton_ref[1]
    gather_ref[1, own[1], rank:] = row_ref[...]
    pl.semaphore_wait(barrier, len(others))

    small = []
    for step, peer in enumerate(peers):
        small.append(
            pltpu.make_async_remote_copy(
                src_ref=parts_ref.at[peer[1]],
                dst_ref=sums_ref.at[step],
                send_sem=small_send.at[step],
                recv_sem=small_recv.at[step],
                device_id=peer,
                device_id_type=MESH,
            )
        )
    for way, other in enumerate((before, after)):
        small.append(
            pltpu.make_async_remote_copy(
                src_ref=edges_ref.at[way],
                dst_ref=halo_ref.at[1 - way],
                send_sem=small_send.at[subs - 1 + way],
                recv_sem=small_recv.at[subs - 1 + way],
                device_id=other,
                device_id_type=MESH,
            )
        )
    for copy in small[: subs - 1]:
        copy.start()

    sent = []

    def near_copy(half, step):
        here = gather_ref.at[half, own[half]]
        return pltpu.make_async_remote_copy(
            src_ref=here,
            dst_ref=here,
            send_sem=near_send.at[half, step],
            recv_sem=near_recv.at[half, step],
            device_id=inner_line[half][step - 1],
            device_id_type=MESH,
        )

    def near_wait(half, step):
        pltpu.make_async_remote_copy(
            src_ref=gather_ref.at[half, own[half]],
            dst_ref=gather_ref.at[half, slot(half, -step, 0)],
            send_sem=near_send.at[half, step],
            recv_sem=near_recv.at[half, step],
            device_id=inner_line[half][step - 1],
            device_id_type=MESH,
        ).wait_recv()

    def slab(half, group, b):
        first = (core * SIDE + wrapped(outer[half], b, SIDE)) * SIDE + group * width
        return gather_ref.at[half, pl.ds(first, width)]

    def slab_copy(half, group, b, way):
        here = slab(half, group, b)
        landed = (b - 1 if way == 0 else b + 1) % SIDE
        return pltpu.make_async_remote_copy(
            src_ref=here,
            dst_ref=here,
            send_sem=slab_send.at[half, group, landed],
            recv_sem=slab_recv.at[half, group, landed],
            device_id=outer_ring[half][way],
            device_id_type=MESH,
        )

    def pair_copy(half, group, b):
        here = slab(half, group, b)
        return pltpu.make_async_remote_copy(
            src_ref=here,
            dst_ref=here,
            send_sem=pair_send.at[half, group, b % SIDE],
            recv_sem=pair_recv.at[half, group, b % SIDE],
            device_id=partner,
            device_id_type=MESH,
        )

    def go(copy):
        copy.start()
        sent.append(copy)

    order = sorted(range(1, SIDE), key=lambda step: -min(step, SIDE - step))
    for step in order:
        go(near_copy(1, step))
    for copy in small[: subs - 1]:
        copy.wait_recv()
    parent = parts_ref[sub]
    for step in range(subs - 1):
        parent = parent + sums_ref[step]
    gather_ref[0, own[0], rank:] = parent
    for copy in small[subs - 1 :]:
        copy.start()
    for step in order:
        go(near_copy(0, step))

    def limit(group, way):
        return reach if group == way else reach - 1

    for half in (1, 0):
        for step in range(1, SIDE):
            near_wait(half, step)
        for way in (0, 1):
            for group in (way, 1 - way):
                go(slab_copy(half, group, 0, way))
        for group in (0, 1):
            go(pair_copy(half, group, 0))
    for step in range(1, reach + 1):
        for half in (1, 0):
            for turn in (0, 1):
                for way in (0, 1):
                    group = way if turn == 0 else 1 - way
                    if step > limit(group, way):
                        continue
                    b = -step if way == 0 else step
                    slab_copy(half, group, b + 1 if way == 0 else b - 1, way).wait_recv()
                    if step < limit(group, way):
                        go(slab_copy(half, group, b, way))
                    go(pair_copy(half, group, b))
    for copy in small:
        copy.wait_send()
    for copy in small[subs - 1 :]:
        copy.wait_recv()
    for half in (1, 0):
        for group in (0, 1):
            for b in range(SIDE):
                pair_copy(half, group, b).wait_recv()

    plane = SIDE * SIDE
    for side in range(CORES):
        parents_ref[:, side] = gather_ref[0, side * plane : (side + 1) * plane, rank:]
    leaves, entries = source_ref.shape[0], source_ref.shape[2] // rank
    lane = lax.broadcasted_iota(jnp.int32, (rank, row_ref.shape[1]), 1)
    for target in range(leaves):
        for entry in range(entries):
            at_0 = where_ref[0, target * entries + entry]
            at_1 = where_ref[1, target * entries + entry]
            low = gather_ref[0, at_0, :rank]
            high = gather_ref[1, at_1, :rank]
            named = jnp.broadcast_to(gather_ref[1, at_1, rank : rank + 1], lane.shape)
            named = jnp.sum(jnp.where(lane == leaf, named, 0.0), axis=1, keepdims=True)
            both = jnp.where(named < 1.5, low, high)
            odd = (named == 1.0) | (named == 3.0)
            source_ref[target, :, entry * rank : (entry + 1) * rank] = jnp.where(
                odd, both[:, rank:], both[:, :rank]
            )
    for copy in sent:
        copy.wait_send()


def exchange(skeleton, row, parts, edges, where, leaves, subs, leaf_total):
    rank = skeleton.shape[1]
    rows = rank + row.shape[0]
    lanes = skeleton.shape[2]
    entries = where.shape[1] // leaves
    vmem = pl.BlockSpec(memory_space=pltpu.VMEM)
    dma = pltpu.SemaphoreType.DMA
    return pl.pallas_call(
        functools.partial(exchange_kernel, subs, leaf_total),
        out_shape=(
            jax.ShapeDtypeStruct((leaves, rank, entries * rank), jnp.float32),
            jax.ShapeDtypeStruct((leaf_total // CORES, CORES, row.shape[0], lanes), jnp.float32),
            jax.ShapeDtypeStruct(edges.shape, jnp.float32),
        ),
        in_specs=[vmem] * 4 + [pl.BlockSpec(memory_space=pltpu.SMEM)],
        out_specs=(vmem, vmem, vmem),
        scratch_shapes=[
            pltpu.VMEM((2, leaf_total, rows, lanes), jnp.float32),
            pltpu.VMEM((subs - 1,) + parts.shape[1:], jnp.float32),
            dma((2, SIDE)),
            dma((2, SIDE)),
            dma((2, 2, SIDE)),
            dma((2, 2, SIDE)),
            dma((2, 2, SIDE)),
            dma((2, 2, SIDE)),
            dma((subs + 1,)),
            dma((subs + 1,)),
        ],
        compiler_params=pltpu.CompilerParams(collective_id=0, has_side_effects=True),
        name="exchange",
    )(skeleton, row, parts, edges, where)


def sum_kernel(subs, in_ref, out_ref, sums_ref, send_sem, recv_sem):
    leaf, sub = lax.axis_index("leaf"), lax.axis_index("sub")
    peers = [(leaf, wrapped(sub, step, subs)) for step in range(1, subs)]
    barrier = pltpu.get_barrier_semaphore()
    for peer in peers:
        pl.semaphore_signal(barrier, inc=1, device_id=peer, device_id_type=MESH)
    pl.semaphore_wait(barrier, subs - 1)
    copies = [
        pltpu.make_async_remote_copy(
            src_ref=in_ref,
            dst_ref=sums_ref.at[step],
            send_sem=send_sem.at[step],
            recv_sem=recv_sem.at[step],
            device_id=peer,
            device_id_type=MESH,
        )
        for step, peer in enumerate(peers)
    ]
    for copy in copies:
        copy.start()
    result = in_ref[...]
    for step, copy in enumerate(copies):
        copy.wait_recv()
        result = result + sums_ref[step]
    out_ref[...] = result
    for copy in copies:
        copy.wait_send()


def sum_over_sub(values, subs):
    vmem = pl.BlockSpec(memory_space=pltpu.VMEM)
    dma = pltpu.SemaphoreType.DMA
    return pl.pallas_call(
        functools.partial(sum_kernel, subs),
        out_shape=jax.ShapeDtypeStruct(values.shape, jnp.float32),
        in_specs=[vmem],
        out_specs=vmem,
        scratch_shapes=[
            pltpu.VMEM((subs - 1,) + values.shape, jnp.float32),
            dma((subs - 1,)),
            dma((subs - 1,)),
        ],
        compiler_params=pltpu.CompilerParams(collective_id=1, has_side_effects=True),
        name="sum_over_sub",
    )(values)


def build_near(points, sides):
    leaves, size = points.shape[1:]
    subs = lax.axis_size("sub")
    total = lax.axis_size("leaf") * subs * leaves
    position = lax.axis_index("leaf") * subs + lax.axis_index("sub")
    all_points = jnp.concatenate([sides[0][:, None], points, sides[1][:, None]], axis=1)
    near_kernels = []
    for side in range(3):
        index = position * leaves + jnp.arange(leaves) + (side - 1)
        present = (index >= 0) & (index < total)
        values = kernel_blocks(all_points[:, side : side + leaves], points, size)
        near_kernels.append(jnp.where(present[:, None, None], values, 0.0))
    return near_kernels


def one_product(field, points, near_kernels, basis, up, down, chosen, top, row, where):
    rhs, leaves, size = field.shape
    rank = basis.shape[1]
    subs = lax.axis_size("sub")
    leaf_total = lax.axis_size("leaf")
    skeleton = jnp.einsum("pla,lra->lpr", field, basis, precision=precise)
    parent_t = jnp.einsum("lpr,lrq->qp", skeleton, up, precision=precise)
    parts = fold(parent_t.reshape(subs, rank // subs, rhs))
    pairs = jnp.concatenate([skeleton[0::2], skeleton[1::2]], axis=-1)
    edges = jnp.stack([field[:, 0], field[:, -1]])
    edges = jnp.concatenate([edges, jnp.stack([points[:, 0], points[:, -1]])], axis=1)
    sources, parents, sides = exchange(pairs, row, parts, edges, where, leaves, subs, leaf_total)
    parents = unfold(parents.reshape(leaf_total, -1, 2 * rank))
    top_part = jnp.einsum("erp,erq->pq", parents, top, precision=precise)
    top_term = unfold(sum_over_sub(fold(top_part), subs))
    padded = jnp.concatenate([sides[0, :rhs, None], field, sides[1, :rhs, None]], axis=1)
    if near_kernels is None:
        near_kernels = build_near(points, sides[:, rhs:])
    near = 0.0
    for side in range(3):
        near = near + jnp.einsum(
            "plb,lba->pla", padded[:, side : side + leaves], near_kernels[side], precision=precise
        )
    far = jnp.einsum("lpm,lmq->lpq", sources, chosen, precision=precise)
    coef = far + jnp.einsum("pr,lrq->lpq", top_term, down, precision=precise)
    return near + jnp.einsum("lpr,lra->pla", coef, basis, precision=precise), near_kernels


def local(
    field, coords, basis, up_transfer, down_transfer, couplings, top_coupling, send_leaf, list_slot, list_block
):
    rhs = field.shape[0]
    leaves, _, size = basis.shape
    points = jnp.pad(coords, ((0, 5), (0, 0))).reshape(8, leaves, size)
    near_kernels = None
    row = jnp.broadcast_to(send_leaf.reshape(1, -1).astype(jnp.float32), (8, send_leaf.size))
    rank = basis.shape[1]
    chosen = couplings[list_block].reshape(leaves, -1, rank)
    flat = list_slot.reshape(-1)
    slot_y, slot_z, slot_core = flat // (SIDE * CORES), (flat // CORES) % SIDE, flat % CORES
    where = jnp.stack(
        [(slot_core * SIDE + slot_y) * SIDE + slot_z, (slot_core * SIDE + slot_z) * SIDE + slot_y]
    )
    current = field.reshape(rhs, leaves, size)
    for repeat in range(2):
        current, near_kernels = one_product(
            current,
            points,
            near_kernels,
            basis,
            up_transfer,
            down_transfer,
            chosen,
            top_coupling[0],
            row,
            where,
        )
    return current.reshape(rhs, leaves * size)


def solution(mesh):
    joined = ("leaf", "sub")
    in_specs = (
        P(None, joined),
        P(None, joined),
        P(joined, None, None),
        P(joined, None, None),
        P(joined, None, None),
        P(joined, None, None),
        P("leaf", None, "sub", None),
        P("leaf", "sub", None, None),
        P(joined, None),
        P(joined, None),
    )
    return jax.shard_map(local, mesh=mesh, in_specs=in_specs, out_specs=P(None, joined), check_vma=False)
```

```python
import functools
import math

import jax
import jax.numpy as jnp
from jax import lax
from jax.experimental import pallas as pl
from jax.experimental.pallas import tpu as pltpu
from jax.sharding import PartitionSpec as P

precise = lax.Precision.HIGH
MESH = pl.DeviceIdType.MESH
SIDE = 8
CORES = 2


def kernel_blocks(sources, targets, leaf_size):
    dist = 0.0
    for component in range(3):
        gap = sources[component][:, :, None] - targets[component][:, None, :]
        dist = dist + gap * gap
    return jnp.exp(-0.5 * dist) * (1.0 / math.sqrt(leaf_size))


def fold(values):
    half = values.shape[-2] // 2
    return jnp.concatenate([values[..., :half, :], values[..., half:, :]], axis=-1)


def unfold(values):
    half = values.shape[-1] // 2
    return jnp.concatenate([values[..., :half], values[..., half:]], axis=-2)


def place():
    leaf = lax.axis_index("leaf")
    return leaf // (SIDE * CORES), (leaf // CORES) % SIDE, leaf % CORES, lax.axis_index("sub")


def leaf_of(y, z, core):
    return (y * SIDE + z) * CORES + core


def wrapped(index, step, size):
    return lax.rem(index + (step + size), size)


def exchange_kernel(
    subs,
    leaf_total,
    skeleton_ref,
    row_ref,
    parts_ref,
    edges_ref,
    where_ref,
    source_ref,
    parents_ref,
    halo_ref,
    gather_ref,
    sums_ref,
    near_send,
    near_recv,
    slab_send,
    slab_recv,
    pair_send,
    pair_recv,
    small_send,
    small_recv,
):
    y, z, core, sub = place()
    leaf = lax.axis_index("leaf")
    rank = skeleton_ref.shape[1]
    reach = SIDE // 2
    width = SIDE // 2
    partner = (leaf_of(y, z, 1 - core), sub)
    y_line = [(leaf_of(wrapped(y, step, SIDE), z, core), sub) for step in range(1, SIDE)]
    z_line = [(leaf_of(y, wrapped(z, step, SIDE), core), sub) for step in range(1, SIDE)]
    peers = [(leaf, wrapped(sub, step, subs)) for step in range(1, subs)]
    position = leaf * subs + sub
    total = leaf_total * subs
    after = wrapped(position, 1, total)
    before = wrapped(position, -1, total)
    after = (after // subs, after % subs)
    before = (before // subs, before % subs)

    barrier = pltpu.get_barrier_semaphore()
    others = [partner] + y_line + z_line + peers + [after, before]
    for other in others:
        pl.semaphore_signal(barrier, inc=1, device_id=other, device_id_type=MESH)

    inner, outer = (z, y), (y, z)
    inner_line = (z_line, y_line)
    outer_ring = ((y_line[0], y_line[-1]), (z_line[0], z_line[-1]))

    def slot(half, a, b):
        return (core * SIDE + wrapped(outer[half], b, SIDE)) * SIDE + wrapped(inner[half], a, SIDE)

    own = (slot(0, 0, 0), slot(1, 0, 0))
    gather_ref[0, own[0], :rank] = skeleton_ref[0]
    gather_ref[1, own[1], :rank] = skeleton_ref[1]
    gather_ref[1, own[1], rank:] = row_ref[...]
    pl.semaphore_wait(barrier, len(others))

    small = []
    for step, peer in enumerate(peers):
        small.append(
            pltpu.make_async_remote_copy(
                src_ref=parts_ref.at[peer[1]],
                dst_ref=sums_ref.at[step],
                send_sem=small_send.at[step],
                recv_sem=small_recv.at[step],
                device_id=peer,
                device_id_type=MESH,
            )
        )
    for way, other in enumerate((before, after)):
        small.append(
            pltpu.make_async_remote_copy(
                src_ref=edges_ref.at[way],
                dst_ref=halo_ref.at[1 - way],
                send_sem=small_send.at[subs - 1 + way],
                recv_sem=small_recv.at[subs - 1 + way],
                device_id=other,
                device_id_type=MESH,
            )
        )
    for copy in small[: subs - 1]:
        copy.start()

    sent = []

    def near_copy(half, step):
        here = gather_ref.at[half, own[half]]
        return pltpu.make_async_remote_copy(
            src_ref=here,
            dst_ref=here,
            send_sem=near_send.at[half, step],
            recv_sem=near_recv.at[half, step],
            device_id=inner_line[half][step - 1],
            device_id_type=MESH,
        )

    def near_wait(half, step):
        pltpu.make_async_remote_copy(
            src_ref=gather_ref.at[half, own[half]],
            dst_ref=gather_ref.at[half, slot(half, -step, 0)],
            send_sem=near_send.at[half, step],
            recv_sem=near_recv.at[half, step],
            device_id=inner_line[half][step - 1],
            device_id_type=MESH,
        ).wait_recv()

    def slab(half, group, b):
        first = (core * SIDE + wrapped(outer[half], b, SIDE)) * SIDE + group * width
        return gather_ref.at[half, pl.ds(first, width)]

    def slab_copy(half, group, b, way):
        here = slab(half, group, b)
        landed = (b - 1 if way == 0 else b + 1) % SIDE
        return pltpu.make_async_remote_copy(
            src_ref=here,
            dst_ref=here,
            send_sem=slab_send.at[half, group, landed],
            recv_sem=slab_recv.at[half, group, landed],
            device_id=outer_ring[half][way],
            device_id_type=MESH,
        )

    def pair_copy(half, group, b):
        here = slab(half, group, b)
        return pltpu.make_async_remote_copy(
            src_ref=here,
            dst_ref=here,
            send_sem=pair_send.at[half, group, b % SIDE],
            recv_sem=pair_recv.at[half, group, b % SIDE],
            device_id=partner,
            device_id_type=MESH,
        )

    def go(copy):
        copy.start()
        sent.append(copy)

    order = sorted(range(1, SIDE), key=lambda step: -min(step, SIDE - step))
    for step in order:
        go(near_copy(1, step))
    for copy in small[: subs - 1]:
        copy.wait_recv()
    parent = parts_ref[sub]
    for step in range(subs - 1):
        parent = parent + sums_ref[step]
    gather_ref[0, own[0], rank:] = parent
    for copy in small[subs - 1 :]:
        copy.start()
    for step in order:
        go(near_copy(0, step))

    def limit(group, way):
        return reach if group == way else reach - 1

    for half in (1, 0):
        for step in range(1, SIDE):
            near_wait(half, step)
        for way in (0, 1):
            for group in (way, 1 - way):
                go(slab_copy(half, group, 0, way))
        for group in (0, 1):
            go(pair_copy(half, group, 0))
    for step in range(1, reach + 1):
        for half in (1, 0):
            for turn in (0, 1):
                for way in (0, 1):
                    group = way if turn == 0 else 1 - way
                    if step > limit(group, way):
                        continue
                    b = -step if way == 0 else step
                    slab_copy(half, group, b + 1 if way == 0 else b - 1, way).wait_recv()
                    if step < limit(group, way):
                        go(slab_copy(half, group, b, way))
                    go(pair_copy(half, group, b))
    for copy in small:
        copy.wait_send()
    for copy in small[subs - 1 :]:
        copy.wait_recv()
    for half in (1, 0):
        for group in (0, 1):
            for b in range(SIDE):
                pair_copy(half, group, b).wait_recv()

    plane = SIDE * SIDE
    for side in range(CORES):
        parents_ref[:, side] = gather_ref[0, side * plane : (side + 1) * plane, rank:]
    leaves, entries = source_ref.shape[0], source_ref.shape[2] // rank
    lane = lax.broadcasted_iota(jnp.int32, row_ref.shape, 1)
    for target in range(leaves):
        for entry in range(entries):
            at_0 = where_ref[0, target * entries + entry]
            at_1 = where_ref[1, target * entries + entry]
            low = gather_ref[0, at_0, :rank]
            high = gather_ref[1, at_1, :rank]
            named = gather_ref[1, at_1, rank:]
            named = jnp.sum(jnp.where(lane == leaf, named, 0.0), axis=1, keepdims=True)
            named = jnp.concatenate([named] * (rank // lane.shape[0]), axis=0)
            both = jnp.where(named < 1.5, low, high)
            odd = (named == 1.0) | (named == 3.0)
            source_ref[target, :, entry * rank : (entry + 1) * rank] = jnp.where(
                odd, both[:, rank:], both[:, :rank]
            )
    for copy in sent:
        copy.wait_send()


def exchange(skeleton, row, parts, edges, where, leaves, subs, leaf_total):
    rank = skeleton.shape[1]
    rows = rank + row.shape[0]
    lanes = skeleton.shape[2]
    entries = where.shape[1] // leaves
    vmem = pl.BlockSpec(memory_space=pltpu.VMEM)
    dma = pltpu.SemaphoreType.DMA
    return pl.pallas_call(
        functools.partial(exchange_kernel, subs, leaf_total),
        out_shape=(
            jax.ShapeDtypeStruct((leaves, rank, entries * rank), jnp.float32),
            jax.ShapeDtypeStruct((leaf_total // CORES, CORES, row.shape[0], lanes), jnp.float32),
            jax.ShapeDtypeStruct(edges.shape, jnp.float32),
        ),
        in_specs=[vmem] * 4 + [pl.BlockSpec(memory_space=pltpu.SMEM)],
        out_specs=(vmem, vmem, vmem),
        scratch_shapes=[
            pltpu.VMEM((2, leaf_total, rows, lanes), jnp.float32),
            pltpu.VMEM((subs - 1,) + parts.shape[1:], jnp.float32),
            dma((2, SIDE)),
            dma((2, SIDE)),
            dma((2, 2, SIDE)),
            dma((2, 2, SIDE)),
            dma((2, 2, SIDE)),
            dma((2, 2, SIDE)),
            dma((subs + 1,)),
            dma((subs + 1,)),
        ],
        compiler_params=pltpu.CompilerParams(collective_id=0, has_side_effects=True),
        name="exchange",
    )(skeleton, row, parts, edges, where)


def sum_kernel(subs, in_ref, out_ref, sums_ref, send_sem, recv_sem):
    leaf, sub = lax.axis_index("leaf"), lax.axis_index("sub")
    peers = [(leaf, wrapped(sub, step, subs)) for step in range(1, subs)]
    barrier = pltpu.get_barrier_semaphore()
    for peer in peers:
        pl.semaphore_signal(barrier, inc=1, device_id=peer, device_id_type=MESH)
    pl.semaphore_wait(barrier, subs - 1)
    copies = [
        pltpu.make_async_remote_copy(
            src_ref=in_ref,
            dst_ref=sums_ref.at[step],
            send_sem=send_sem.at[step],
            recv_sem=recv_sem.at[step],
            device_id=peer,
            device_id_type=MESH,
        )
        for step, peer in enumerate(peers)
    ]
    for copy in copies:
        copy.start()
    result = in_ref[...]
    for step, copy in enumerate(copies):
        copy.wait_recv()
        result = result + sums_ref[step]
    out_ref[...] = result
    for copy in copies:
        copy.wait_send()


def sum_over_sub(values, subs):
    vmem = pl.BlockSpec(memory_space=pltpu.VMEM)
    dma = pltpu.SemaphoreType.DMA
    return pl.pallas_call(
        functools.partial(sum_kernel, subs),
        out_shape=jax.ShapeDtypeStruct(values.shape, jnp.float32),
        in_specs=[vmem],
        out_specs=vmem,
        scratch_shapes=[
            pltpu.VMEM((subs - 1,) + values.shape, jnp.float32),
            dma((subs - 1,)),
            dma((subs - 1,)),
        ],
        compiler_params=pltpu.CompilerParams(collective_id=1, has_side_effects=True),
        name="sum_over_sub",
    )(values)


def build_near(points, sides):
    leaves, size = points.shape[1:]
    subs = lax.axis_size("sub")
    total = lax.axis_size("leaf") * subs * leaves
    position = lax.axis_index("leaf") * subs + lax.axis_index("sub")
    all_points = jnp.concatenate([sides[0][:, None], points, sides[1][:, None]], axis=1)
    near_kernels = []
    for side in range(3):
        index = position * leaves + jnp.arange(leaves) + (side - 1)
        present = (index >= 0) & (index < total)
        values = kernel_blocks(all_points[:, side : side + leaves], points, size)
        near_kernels.append(jnp.where(present[:, None, None], values, 0.0))
    return near_kernels


def one_product(field, points, near_kernels, basis, up, down, chosen, top, row, where):
    rhs, leaves, size = field.shape
    rank = basis.shape[1]
    subs = lax.axis_size("sub")
    leaf_total = lax.axis_size("leaf")
    skeleton = jnp.einsum("pla,lra->lpr", field, basis, precision=precise)
    parent_t = jnp.einsum("lpr,lrq->qp", skeleton, up, precision=precise)
    parts = fold(parent_t.reshape(subs, rank // subs, rhs))
    pairs = jnp.concatenate([skeleton[0::2], skeleton[1::2]], axis=-1)
    edges = jnp.stack([field[:, 0], field[:, -1]])
    edges = jnp.concatenate([edges, jnp.stack([points[:, 0], points[:, -1]])], axis=1)
    sources, parents, sides = exchange(pairs, row, parts, edges, where, leaves, subs, leaf_total)
    parents = unfold(parents.reshape(leaf_total, -1, 2 * rank))
    top_part = jnp.einsum("erp,erq->pq", parents, top, precision=precise)
    top_term = unfold(sum_over_sub(fold(top_part), subs))
    padded = jnp.concatenate([sides[0, :rhs, None], field, sides[1, :rhs, None]], axis=1)
    if near_kernels is None:
        near_kernels = build_near(points, sides[:, rhs:])
    near = 0.0
    for side in range(3):
        near = near + jnp.einsum(
            "plb,lba->pla", padded[:, side : side + leaves], near_kernels[side], precision=precise
        )
    far = jnp.einsum("lpm,lmq->lpq", sources, chosen, precision=precise)
    coef = far + jnp.einsum("pr,lrq->lpq", top_term, down, precision=precise)
    return near + jnp.einsum("lpr,lra->pla", coef, basis, precision=precise), near_kernels


def local(
    field, coords, basis, up_transfer, down_transfer, couplings, top_coupling, send_leaf, list_slot, list_block
):
    rhs = field.shape[0]
    leaves, _, size = basis.shape
    points = jnp.pad(coords, ((0, 5), (0, 0))).reshape(8, leaves, size)
    near_kernels = None
    row = jnp.broadcast_to(send_leaf.reshape(1, -1).astype(jnp.float32), (8, send_leaf.size))
    rank = basis.shape[1]
    chosen = couplings[list_block].reshape(leaves, -1, rank)
    flat = list_slot.reshape(-1)
    slot_y, slot_z, slot_core = flat // (SIDE * CORES), (flat // CORES) % SIDE, flat % CORES
    where = jnp.stack(
        [(slot_core * SIDE + slot_y) * SIDE + slot_z, (slot_core * SIDE + slot_z) * SIDE + slot_y]
    )
    current = field.reshape(rhs, leaves, size)
    for repeat in range(2):
        current, near_kernels = one_product(
            current,
            points,
            near_kernels,
            basis,
            up_transfer,
            down_transfer,
            chosen,
            top_coupling[0],
            row,
            where,
        )
    return current.reshape(rhs, leaves * size)


def solution(mesh):
    joined = ("leaf", "sub")
    in_specs = (
        P(None, joined),
        P(None, joined),
        P(joined, None, None),
        P(joined, None, None),
        P(joined, None, None),
        P(joined, None, None),
        P("leaf", None, "sub", None),
        P("leaf", "sub", None, None),
        P(joined, None),
        P(joined, None),
    )
    return jax.shard_map(local, mesh=mesh, in_specs=in_specs, out_specs=P(None, joined), check_vma=False)
```
